32 devices in a mesh: dp: 8 (over z, x), tensor: 4 (over y, core).
Axes of the slice: x: 2, y: 2, z: 4, core: 2. Of those that a mesh axis runs over, the one named last changes fastest.
Arguments:
- tokens: bfloat16 [16, 1024, 1536], P('dp', 'tensor'), may hold values from -6 to 6
- cotangent: bfloat16 [16, 1024, 1536], P('dp', 'tensor'), may hold values from -6 to 6
- lengths: int32 [16], replicated, may hold values from 1 to 1024, 10240 in all
- order: int32 [16], replicated, may hold values from 0 to 15, each once
- proj_gate: bfloat16 [1536, 3072], P('dp', 'tensor'), may hold values from -0.15625 to 0.15625
- proj_values: bfloat16 [1536, 3072], P('dp', 'tensor'), may hold values from -0.15625 to 0.15625
- proj_delta: bfloat16 [1536, 48], P('dp', 'tensor'), may hold values from -0.15625 to 0.15625
- proj_state: bfloat16 [1536, 256], P('dp'), may hold values from -0.0390625 to 0.0390625
- proj_out: bfloat16 [1536, 3072], P('dp', 'tensor'), may hold values from -0.109375 to 0.109375
- pre_gain: float32 [1536], replicated, may hold values from 0.1 to 1.9
- gate_gain: float32 [3072], P('tensor'), may hold values from 0.1 to 1.9
- value_conv: float32 [3072, 4], P('tensor'), may hold values from -3 to 3
- value_shift: float32 [3072], P('tensor'), may hold values from -3 to 3
- state_conv: float32 [256, 4], replicated, may hold values from -3 to 3
- state_shift: float32 [256], replicated, may hold values from -1.5 to 1.5
- delta_bias: float32 [48], P('tensor'), may hold values from -6 to -2
- decay_log: float32 [48], P('tensor'), may hold values from 0 to 2.7
- skip_gain: float32 [48], P('tensor'), may hold values from 0 to 2
Outputs:
- out_tokens: bfloat16 [16, 1024, 1536], P('dp', 'tensor')
- grad_tokens: bfloat16 [16, 1024, 1536], P('dp', 'tensor')
- grad_proj_gate: float32 [1536, 3072], P('dp', 'tensor')
- grad_proj_values: float32 [1536, 3072], P('dp', 'tensor')
- grad_proj_delta: float32 [1536, 48], P('dp', 'tensor')
- grad_proj_state: float32 [1536, 256], P('dp')
- grad_proj_out: float32 [1536, 3072], P('dp', 'tensor')
- grad_pre_gain: float32 [1536], replicated
- grad_gate_gain: float32 [3072], replicated
- grad_value_conv: float32 [3072, 4], replicated
- grad_value_shift: float32 [3072], replicated
- grad_state_conv: float32 [256, 4], replicated
- grad_state_shift: float32 [256], replicated
- grad_delta_bias: float32 [48], replicated
- grad_decay_log: float32 [48], replicated
- grad_skip_gain: float32 [48], replicated
The draws below stay inside these ranges and needn't reach their ends.
Inputs may be any that keep to these rules, and one draw needn't show every extreme that they name: `lengths`: each slot holds 1 or more real tokens at its start, the rest padding; the largest is exactly 1024, and together they fill five eighths of 16384 positions. `order`: each slot number appears exactly once.
All inputs are finite; a program needn't handle non-finite values.
Results may differ from the reference program's by a relative error of at most 0.0095.
Values may be sent and summed in bfloat16 or wider, within the bound.
No kernel may reach another device: no remote copies, remote signals or barrier semaphores. Data moves between devices by JAX's collectives and lax.ppermute only.
A program may use at most 192 MiB of HBM per device.

```python
import math
import jax
import jax.numpy as jnp
import numpy as np
from jax import lax

D = 1536
HEADS = 48
STATE = 128
CONV = 4
BLOCK = 256
SEQ = 1024
INNER = 3072
SLOTS = 16


def level_of(rng, shape, shards, smallest, largest):
    level, own = 1.0, jax.random.fold_in(rng, 6)
    for position, parts in shards:
        steps = jnp.exp(jax.random.uniform(jax.random.fold_in(own, position), (parts,), jnp.float32, smallest / len(shards), largest / len(shards)))
        level = level * jnp.repeat(steps, shape[position] // parts).reshape([-1 if axis == position else 1 for axis in range(len(shape))])
    return level


def length_profile(amount, total, most, slope):
    portions = [(1 << 20) // math.isqrt(standing ** slope) + 1 for standing in range(2, amount + 1)]
    surplus, given = total - most - (amount - 1), [1] * (amount - 1)
    while surplus > 0:
        candidates = [i for i in range(amount - 1) if given[i] < most]
        whole, budget = sum([portions[i] for i in candidates]), surplus
        for i in candidates:
            more = min(most - given[i], max(1, budget * portions[i] // whole), surplus)
            given[i] = given[i] + more
            surplus = surplus - more
    return np.array([most] + given)


def uneven_parts(own_key, count, total, limit, skew):
    if count == 2:
        one = jax.random.randint(own_key, (), max(1, total - limit), min(limit, total - 1) + 1)
        return jnp.stack([one, total - one])
    tallies = jnp.asarray(length_profile(count, total, limit, skew), jnp.int32)
    couples = (count - 1) // 2
    donor, receiver = tallies[1:1 + 2 * couples:2], tallies[2:2 + 2 * couples:2]
    margin = jnp.minimum(donor - 1, limit - receiver)
    moved = jax.random.randint(jax.random.fold_in(own_key, 1), (couples,), 0, 1 << 20) % (margin + 1)
    tallies = tallies.at[1:1 + 2 * couples:2].set(donor - moved).at[2:2 + 2 * couples:2].set(receiver + moved)
    return tallies[jax.random.permutation(jax.random.fold_in(own_key, 2), count)]


def scatter_about(stream_key, shape, deviation, bound, shards=(), kind=jnp.bfloat16):
    factor_of = level_of(stream_key, shape, shards, -0.22, 0.18) if shards else 1.0
    values = jax.random.normal(stream_key, shape, jnp.float32) * deviation * factor_of
    return jnp.minimum(jnp.maximum(values, -bound), bound).astype(kind)


def setup_inputs(seed: int = 0) -> dict:
    splits = jax.random.split(jax.random.key(seed), 19)
    tokens = scatter_about(splits[0], (SLOTS, SEQ, D), 1.0, 6.0, ((0, 8), (1, 4)))
    cotangent = scatter_about(splits[1], (SLOTS, SEQ, D), 1.0, 6.0, ((0, 8), (1, 4)))
    lengths = uneven_parts(splits[2], SLOTS, SLOTS * SEQ * 5 // 8, SEQ, 2).astype(jnp.int32)
    order = jax.random.permutation(splits[3], SLOTS).astype(jnp.int32)
    proj_gate = scatter_about(splits[4], (D, INNER), D ** -0.5, 0.15625, ((0, 8), (1, 4)))
    proj_values = scatter_about(splits[5], (D, INNER), D ** -0.5, 0.15625, ((0, 8), (1, 4)))
    proj_delta = scatter_about(splits[6], (D, HEADS), D ** -0.5, 0.15625, ((0, 8), (1, 4)))
    proj_state = scatter_about(splits[7], (D, 2 * STATE), (16 * D) ** -0.5, 0.0390625, ((0, 8),))
    proj_out = scatter_about(splits[8], (D, INNER), INNER ** -0.5, 0.109375, ((0, 8), (1, 4)))
    pre_gain = jnp.clip(1.0 + 0.18 * jax.random.normal(splits[9], (D,), jnp.float32), 0.1, 1.9)
    gate_gain = jnp.clip(1.0 + 0.18 * jax.random.normal(splits[10], (INNER,), jnp.float32), 0.1, 1.9)
    value_conv = scatter_about(splits[11], (INNER, CONV), CONV ** -0.5, 3.0, ((0, 4),), jnp.float32)
    value_shift = scatter_about(splits[12], (INNER,), 0.5, 3.0, ((0, 4),), jnp.float32)
    state_conv = scatter_about(splits[13], (2 * STATE, CONV), CONV ** -0.5, 3.0, (), jnp.float32)
    state_shift = scatter_about(splits[14], (2 * STATE,), 0.25, 1.5, (), jnp.float32)
    delta_bias = jnp.clip(-6.0 + 4.0 * jax.random.uniform(splits[15], (HEADS,), jnp.float32) ** level_of(splits[15], (HEADS,), ((0, 4),), -0.2, 0.2), -6.0, -2.0)
    decay_log = jnp.clip(2.7 * jax.random.uniform(splits[16], (HEADS,), jnp.float32) ** level_of(splits[16], (HEADS,), ((0, 4),), -0.2, 0.2), 0.0, 2.7)
    skip_gain = jnp.clip(2.0 * jax.random.uniform(splits[17], (HEADS,), jnp.float32) ** level_of(splits[17], (HEADS,), ((0, 4),), -0.2, 0.2), 0.0, 2.0)
    return {"tokens": tokens, "cotangent": cotangent, "lengths": lengths, "order": order, "proj_gate": proj_gate, "proj_values": proj_values, "proj_delta": proj_delta, "proj_state": proj_state, "proj_out": proj_out, "pre_gain": pre_gain, "gate_gain": gate_gain, "value_conv": value_conv, "value_shift": value_shift, "state_conv": state_conv, "state_shift": state_shift, "delta_bias": delta_bias, "decay_log": decay_log, "skip_gain": skip_gain}


norm_eps = 1e-05
highest = lax.Precision.HIGHEST

@jax.custom_vjp
def low(v):
    return lax.optimization_barrier(v.astype(jnp.bfloat16)).astype(jnp.float32)

@jax.custom_vjp
def low_back(v):
    return v

def low_keep(v):
    return (low(v), None)

def low_pass(kept, grad):
    return (grad,)

def back_keep(v):
    return (v, None)

def back_low(kept, grad):
    return (low(grad),)
low.defvjp(low_keep, low_pass)
low_back.defvjp(back_keep, back_low)

def causal_conv(values, weights, shift):
    reach = weights.shape[1]
    length = values.shape[0]
    padded = jnp.pad(values, ((reach - 1, 0), (0, 0)))
    total = jnp.zeros_like(values) + shift[None, :]
    for offset in range(reach):
        total = total + weights[:, offset][None, :] * padded[offset:offset + length]
    return total

def state_mixer(value_in, state_in, delta_in, value_conv, value_shift, state_conv, state_shift, delta_bias, decay_log, skip_gain):
    length = value_in.shape[0]
    heads = delta_bias.shape[0]
    head_width = value_in.shape[1] // heads
    state_width = state_in.shape[1] // 2
    blocks = length // BLOCK
    values = jax.nn.silu(causal_conv(value_in, value_conv, value_shift))
    state_act = jax.nn.silu(causal_conv(state_in, state_conv, state_shift))
    delta = jax.nn.softplus(delta_in + delta_bias[None, :])
    rates = -jnp.exp(decay_log)
    values = values.reshape(blocks, BLOCK, heads, head_width)
    inputs = state_act[:, :state_width].reshape(blocks, BLOCK, state_width)
    readout = state_act[:, state_width:].reshape(blocks, BLOCK, state_width)
    delta_blocks = delta.reshape(blocks, BLOCK, heads)
    cumul = jnp.cumsum(delta_blocks * rates[None, None, :], axis=1)
    lower = (jnp.arange(BLOCK)[:, None] >= jnp.arange(BLOCK)[None, :])[None, :, :, None]
    gaps = cumul[:, :, None, :] - cumul[:, None, :, :]
    decay_mat = jnp.exp(jnp.where(lower, gaps, -10000.0))
    intersection = jnp.einsum('bin,bjn->bij', readout, inputs, precision=highest)
    weighted = values * delta_blocks[..., None]
    mixing = intersection[..., None] * decay_mat
    inner_out = jnp.einsum('bijh,bjhp->bihp', mixing, weighted, precision=highest)
    to_end = jnp.exp(cumul[:, -1:, :] - cumul)
    block_states = jnp.einsum('bjhp,bjn->bhpn', weighted * to_end[..., None], inputs, precision=highest)
    block_decay = jnp.exp(cumul[:, -1, :])
    carried = []
    running = jnp.zeros((heads, head_width, state_width), jnp.float32)
    for index in range(blocks):
        carried.append(running)
        running = block_decay[index][:, None, None] * running + block_states[index]
    starts = jnp.stack(carried)
    cross_out = jnp.einsum('bin,bhpn->bihp', readout, starts, precision=highest) * jnp.exp(cumul)[..., None]
    result = inner_out + cross_out + skip_gain[None, None, :, None] * values
    return result.reshape(length, heads * head_width)

def block_forward(params, rows_in, valid_len):
    proj_gate, proj_values, proj_delta, proj_state, proj_out, pre_gain, gate_gain, value_conv, value_shift, state_conv, state_shift, delta_bias, decay_log, skip_gain = params
    scale = lax.rsqrt(lax.optimization_barrier(jnp.mean(rows_in * rows_in, axis=-1, keepdims=True)) + norm_eps)
    normed = low(rows_in * scale * pre_gain[None, :])
    gate_in = low_back(jnp.dot(normed, proj_gate, precision=highest))
    value_in = low_back(jnp.dot(normed, proj_values, precision=highest))
    delta_in = low_back(jnp.dot(normed, proj_delta, precision=highest))
    state_in = low_back(jnp.dot(normed, proj_state, precision=highest))
    mixed = state_mixer(value_in, state_in, delta_in, value_conv, value_shift, state_conv, state_shift, delta_bias, decay_log, skip_gain)
    gated = mixed * jax.nn.silu(gate_in)
    gate_scale = lax.rsqrt(lax.optimization_barrier(jnp.mean(gated * gated, axis=-1, keepdims=True)) + norm_eps)
    hidden = low(gated * gate_scale * gate_gain[None, :])
    branch = jnp.dot(hidden, proj_out.T, precision=highest)
    valid = (jnp.arange(rows_in.shape[0], dtype=jnp.int32) < valid_len).astype(jnp.float32)[:, None]
    return rows_in + valid * branch

def reference(tokens, cotangent, lengths, order, proj_gate, proj_values, proj_delta, proj_state, proj_out, pre_gain, gate_gain, value_conv, value_shift, state_conv, state_shift, delta_bias, decay_log, skip_gain):
    params = tuple((item.astype(jnp.float32) for item in (proj_gate, proj_values, proj_delta, proj_state, proj_out, pre_gain, gate_gain, value_conv, value_shift, state_conv, state_shift, delta_bias, decay_log, skip_gain)))
    zero_grads = jax.tree.map(jnp.zeros_like, params)

    def per_slot(carry, slot):
        source = order[slot]
        block_in = lax.dynamic_index_in_dim(tokens, source, 0, keepdims=False).astype(jnp.float32)
        valid_len = lengths[source]

        def slot_forward(weights, rows_in):
            return block_forward(weights, rows_in, valid_len)
        out_block, pullback = jax.vjp(slot_forward, params, block_in)
        out_grad = lax.dynamic_index_in_dim(cotangent, slot, 0, keepdims=False).astype(jnp.float32)
        grad_params, grad_in = pullback(out_grad)
        carry = jax.tree.map(jnp.add, carry, grad_params)
        return (carry, (out_block.astype(jnp.bfloat16), grad_in.astype(jnp.bfloat16)))
    grads, (outputs, in_grads) = lax.scan(per_slot, zero_grads, jnp.arange(SLOTS, dtype=jnp.int32))
    home = jnp.zeros_like(in_grads).at[order].set(in_grads)
    return (outputs, home) + tuple(grads)
```

```python
import functools
import jax
import jax.numpy as jnp
from jax import lax
from jax.experimental import pallas as pl
from jax.experimental.pallas import tpu as pltpu
from jax.sharding import PartitionSpec as P

LANES = 128
CHUNK = 128
F32 = jnp.float32
BF16 = jnp.bfloat16
HI = lax.Precision.HIGHEST
norm_eps = 1e-05


def dot(a, b, precision=None):
    return lax.dot_general(a, b, (((1,), (0,)), ((), ())), precision=precision,
                           preferred_element_type=F32)


def dot_nt(a, b, precision=None):
    return lax.dot_general(a, b, (((1,), (1,)), ((), ())), precision=precision,
                           preferred_element_type=F32)


def iota2(axis):
    return lax.broadcasted_iota(jnp.int32, (CHUNK, LANES), axis)


def conv_tile(buf, row, taps_ref, shift_ref, lanes):
    total = jnp.broadcast_to(shift_ref[:, lanes], (CHUNK, LANES))
    for k in range(4):
        total = total + taps_ref[k:k + 1, lanes] * buf[row + 5 + k:row + 5 + k + CHUNK, lanes]
    return total


def sigmoid(v):
    return 1.0 / (1.0 + jnp.exp(-v))


def softplus(v):
    return jnp.maximum(v, 0.0) + jnp.log(1.0 + jnp.exp(-jnp.abs(v)))


def pair_lanes(q, hp, low_half):
    return jnp.where(low_half, q[:, 2 * hp:2 * hp + 1], q[:, 2 * hp + 1:2 * hp + 2])


def decays(delta_in, bias_ref, rate_ref, lower):
    v = delta_in + bias_ref[...]
    delta = softplus(v)
    a = delta * rate_ref[...]
    cum = dot(lower.astype(F32), a, HI)
    last = cum[CHUNK - 1:CHUNK, :]
    return v, delta, a, cum, jnp.exp(cum), jnp.exp(last - cum), jnp.exp(last)


def forward_kernel(pairs, rows, perm_ref, vsd_ref, gate_ref, taps_ref, shift_ref, bias_ref,
                   rate_ref, skip_ref, gain_ref, mixed_ref, hid_ref, sq_ref, st_ref, buf, state):
    width = pairs * LANES
    step = pl.program_id(1)

    @pl.when(step == 0)
    def _():
        buf[0:8, :] = jnp.zeros((8, width + 2 * LANES), F32)
        state[...] = jnp.zeros_like(state)

    buf[8:8 + rows, :] = vsd_ref[:, 0:width + 2 * LANES]
    row_i, col_j = iota2(0), iota2(1)
    lower = row_i >= col_j
    low_half = col_j < LANES // 2
    for sub in range(rows // CHUNK):
        r0 = sub * CHUNK
        rs = slice(r0, r0 + CHUNK)
        pre_b = conv_tile(buf, r0, taps_ref, shift_ref, slice(width, width + LANES))
        pre_c = conv_tile(buf, r0, taps_ref, shift_ref, slice(width + LANES, width + 2 * LANES))
        b_act = pre_b * sigmoid(pre_b)
        c_low = (pre_c * sigmoid(pre_c)).astype(BF16)
        b_low = b_act.astype(BF16)
        b_t = b_act.T.astype(BF16)
        _, delta, _, cum, eq, te, eq_last = decays(
            vsd_ref[rs, width + 2 * LANES:width + 3 * LANES], bias_ref, rate_ref, lower)
        cum_t = cum.T
        cb = dot_nt(c_low, b_low)
        squares = jnp.zeros((CHUNK, LANES), F32)
        for hp in range(pairs):
            lanes = slice(hp * LANES, hp * LANES + LANES)
            pre = conv_tile(buf, r0, taps_ref, shift_ref, lanes)
            x = pre * sigmoid(pre)
            xw = x * pair_lanes(delta, hp, low_half)
            mix = []
            for h in (2 * hp, 2 * hp + 1):
                gap = jnp.where(lower, cum[:, h:h + 1] - cum_t[h:h + 1, :], -10000.0)
                mix.append((cb * jnp.exp(gap)).astype(BF16))
            mix = jnp.concatenate(mix, axis=1)
            xw2 = jnp.concatenate([jnp.where(low_half, xw, 0.0), jnp.where(low_half, 0.0, xw)],
                                  axis=0).astype(BF16)
            st = state[:, lanes]
            st_low = st.astype(BF16)
            st_ref[sub, :, lanes] = st_low
            y = (dot(mix, xw2) + dot(c_low, st_low) * pair_lanes(eq, hp, low_half)
                 + skip_ref[:, lanes] * x)
            state[:, lanes] = (st * pair_lanes(eq_last, hp, low_half[0:1])
                               + dot(b_t, (xw * pair_lanes(te, hp, low_half)).astype(BF16)))
            mixed_ref[rs, lanes] = y
            gate = gate_ref[rs, lanes]
            gated = y * (gate * sigmoid(gate))
            hid_ref[rs, lanes] = (gated * gain_ref[:, lanes]).astype(BF16)
            squares = squares + gated * gated
        sq_ref[8 * sub:8 * sub + 8, :] = dot_nt(jnp.ones((8, LANES), F32), squares, HI)
    buf[0:8, :] = buf[rows:rows + 8, :]


def row_spec(rows, width, where):
    return pl.BlockSpec((rows, width), where)


def const_spec(shape):
    return pl.BlockSpec(shape, lambda s, i, perm: (0,) * len(shape))


def mixer_forward(perm, slots, vsd, gate_in, taps, shift, bias, rate, skip, gain):
    seq, width = gate_in.shape
    pairs = width // LANES
    parts = perm.shape[0]
    rows = seq // parts // slots
    subs = rows // CHUNK
    here = lambda s, i, perm: (perm[i] * slots + s, 0)
    return pl.pallas_call(
        functools.partial(forward_kernel, pairs, rows),
        grid_spec=pltpu.PrefetchScalarGridSpec(
            num_scalar_prefetch=1,
            grid=(slots, parts),
            in_specs=[
                row_spec(rows, width + 3 * LANES, here),
                row_spec(rows, width, here),
                const_spec(taps.shape), const_spec(shift.shape), const_spec(bias.shape),
                const_spec(rate.shape), const_spec(skip.shape), const_spec(gain.shape),
            ],
            out_specs=[
                row_spec(rows, width, here),
                row_spec(rows, width, here),
                row_spec(8 * subs, LANES, here),
                pl.BlockSpec((subs, LANES, width), lambda s, i, perm: (s * parts + i, 0, 0)),
            ],
            scratch_shapes=[
                pltpu.VMEM((8 + rows, width + 2 * LANES), F32),
                pltpu.VMEM((LANES, width), F32),
            ],
        ),
        out_shape=[
            jax.ShapeDtypeStruct((seq, width), F32),
            jax.ShapeDtypeStruct((seq, width), BF16),
            jax.ShapeDtypeStruct((seq // CHUNK * 8, LANES), F32),
            jax.ShapeDtypeStruct((seq // CHUNK, LANES, width), BF16),
        ],
        cost_estimate=pl.CostEstimate(flops=seq * width * 6000, bytes_accessed=seq * width * 16,
                                      transcendentals=seq * width * 4),
        name="mixer_forward",
    )(perm, vsd, gate_in, taps, shift, bias, rate, skip, gain)


def backward_kernel(pairs, rows, parts, perm_ref, vsd_ref, halo_ref, gm_ref, st_ref, taps_ref,
                    shift_ref, bias_ref, rate_ref, skip_ref, low_ref, wide_ref, head_ref,
                    buf, gbuf, dstate, taps_acc, skip_acc, head_acc):
    width = pairs * LANES
    full = width + 2 * LANES
    step = pl.program_id(1)
    first = jnp.logical_and(step == 0, pl.program_id(0) == 0)
    last = jnp.logical_and(step == parts - 1, pl.program_id(0) == pl.num_programs(0) - 1)
    subs = rows // CHUNK

    @pl.when(step == 0)
    def _():
        gbuf[rows:rows + 8, :] = jnp.zeros((8, full), F32)
        dstate[...] = jnp.zeros_like(dstate)

    @pl.when(first)
    def _():
        taps_acc[...] = jnp.zeros_like(taps_acc)
        skip_acc[...] = jnp.zeros_like(skip_acc)
        head_acc[...] = jnp.zeros_like(head_acc)

    buf[8:8 + rows, :] = vsd_ref[:, 0:full]
    buf[0:8, :] = jnp.where(step == parts - 1, 0.0, halo_ref[:, 0:full])
    row_i, col_j = iota2(0), iota2(1)
    lower = row_i >= col_j
    upper = col_j >= row_i
    strict = row_i > col_j
    low_half = col_j < LANES // 2
    for sub in reversed(range(subs)):
        r0 = sub * CHUNK
        rs = slice(r0, r0 + CHUNK)
        pre_b = conv_tile(buf, r0, taps_ref, shift_ref, slice(width, width + LANES))
        pre_c = conv_tile(buf, r0, taps_ref, shift_ref, slice(width + LANES, full))
        sig_b = sigmoid(pre_b)
        sig_c = sigmoid(pre_c)
        b_low = (pre_b * sig_b).astype(BF16)
        c_act = pre_c * sig_c
        c_low = c_act.astype(BF16)
        c_t = c_act.T.astype(BF16)
        v, delta, a, cum, eq, te, eq_last = decays(
            vsd_ref[rs, full:full + LANES], bias_ref, rate_ref, lower)
        cum_t = cum.T
        bc = dot_nt(b_low, c_low)
        d_bc = jnp.zeros((CHUNK, LANES), F32)
        g_b = jnp.zeros((CHUNK, LANES), F32)
        g_c = jnp.zeros((CHUNK, LANES), F32)
        sums = jnp.zeros((3 * CHUNK + 8, LANES), F32)
        col_sum = jnp.zeros((CHUNK, LANES), F32)
        row_sum = jnp.zeros((CHUNK, LANES), F32)
        for hp in range(pairs):
            lanes = slice(hp * LANES, hp * LANES + LANES)
            pre = conv_tile(buf, r0, taps_ref, shift_ref, lanes)
            sig = sigmoid(pre)
            x = pre * sig
            d_lane = pair_lanes(delta, hp, low_half)
            te_lane = pair_lanes(te, hp, low_half)
            xw = x * d_lane
            g = gm_ref[rs, lanes]
            g_low = g.astype(BF16)
            xw2 = jnp.concatenate([jnp.where(low_half, xw, 0.0), jnp.where(low_half, 0.0, xw)],
                                  axis=0).astype(BF16)
            g2 = jnp.concatenate([jnp.where(low_half, g, 0.0), jnp.where(low_half, 0.0, g)],
                                 axis=0).astype(BF16)
            d_mix = dot_nt(xw2, g_low)
            mix = []
            for side, h in enumerate((2 * hp, 2 * hp + 1)):
                gap = jnp.where(upper, cum_t[h:h + 1, :] - cum[:, h:h + 1], -10000.0)
                e = jnp.exp(gap)
                m = bc * e
                mix.append(m.astype(BF16))
                d_m = d_mix[side * CHUNK:side * CHUNK + CHUNK, :]
                d_bc = d_bc + d_m * e
                p = d_m * m
                col_sum = jnp.where(col_j == h, jnp.sum(p, axis=1, keepdims=True), col_sum)
                row_sum = jnp.where(row_i == h, jnp.sum(p, axis=0, keepdims=True), row_sum)
            st = st_ref[sub, :, lanes]
            ds = dstate[:, lanes]
            ds_low = ds.astype(BF16)
            g_eq = g * pair_lanes(eq, hp, low_half)
            g_eq_low = g_eq.astype(BF16)
            xw_te = xw * te_lane
            b_ds = dot(b_low, ds_low)
            d_xw = dot(jnp.concatenate(mix, axis=1), g2) + te_lane * b_ds
            prod = ds * st.astype(F32)
            prod = sum(prod[8 * i:8 * i + 8] for i in range(LANES // 8))
            terms = jnp.concatenate([g_eq * dot(c_low, st), xw_te * b_ds, x * d_xw, prod], axis=0)
            place = jnp.where(col_j == 2 * hp + (row_i >= LANES // 2).astype(jnp.int32), 1.0, 0.0)
            sums = sums + dot(terms.astype(BF16), place.astype(BF16))
            g_c = g_c + dot_nt(g_eq_low, st)
            g_b = g_b + dot_nt(xw_te.astype(BF16), ds_low)
            dstate[:, lanes] = (ds * pair_lanes(eq_last, hp, low_half[0:1])
                                + dot(c_t, g_eq_low))
            g_x = d_lane * d_xw + skip_ref[:, lanes] * g
            gx = g * x
            skip_acc[:, lanes] += sum(gx[8 * i:8 * i + 8] for i in range(CHUNK // 8))
            gbuf[rs, lanes] = g_x * (sig * (1.0 + pre * (1.0 - sig)))
        d_bc_t = d_bc.T.astype(BF16)
        g_b = g_b + dot(d_bc.astype(BF16), c_low)
        g_c = g_c + dot(d_bc_t, b_low)
        gbuf[rs, width:width + LANES] = g_b * (sig_b * (1.0 + pre_b * (1.0 - sig_b)))
        gbuf[rs, width + LANES:full] = g_c * (sig_c * (1.0 + pre_c * (1.0 - sig_c)))
        g_cum = row_sum.T - col_sum + sums[0:CHUNK]
        inner = jnp.sum(sums[3 * CHUNK:3 * CHUNK + 8], axis=0, keepdims=True)
        g_a = (dot(upper.astype(F32), g_cum, HI) + dot(strict.astype(F32), sums[CHUNK:2 * CHUNK], HI)
               + eq_last * inner)
        g_delta = sums[2 * CHUNK:3 * CHUNK] + rate_ref[...] * g_a
        g_din = g_delta * sigmoid(v)
        low_ref[rs, full:full + LANES] = g_din.astype(BF16)
        a_ga = a * g_a
        head_acc[0:8] += sum(g_din[8 * i:8 * i + 8] for i in range(CHUNK // 8))
        head_acc[8:16] += sum(a_ga[8 * i:8 * i + 8] for i in range(CHUNK // 8))
    for tile in range(full // LANES):
        lanes = slice(tile * LANES, tile * LANES + LANES)
        for sub in range(subs):
            r0 = sub * CHUNK
            g_in = jnp.zeros((CHUNK, LANES), F32)
            g_pre = gbuf[r0:r0 + CHUNK, lanes]
            for k in range(4):
                g_in = g_in + taps_ref[k:k + 1, lanes] * gbuf[r0 + 3 - k:r0 + 3 - k + CHUNK, lanes]
                t = g_pre * buf[r0 + 5 + k:r0 + 5 + k + CHUNK, lanes]
                taps_acc[8 * k:8 * k + 8, lanes] += sum(t[8 * i:8 * i + 8] for i in range(CHUNK // 8))
            taps_acc[32:40, lanes] += sum(g_pre[8 * i:8 * i + 8] for i in range(CHUNK // 8))
            low_ref[r0:r0 + CHUNK, lanes] = g_in.astype(BF16)
    gbuf[rows:rows + 8, :] = gbuf[0:8, :]

    @pl.when(last)
    def _():
        wide_ref[...] = jnp.zeros_like(wide_ref)
        for k in range(5):
            wide_ref[k:k + 1, :] = jnp.sum(taps_acc[8 * k:8 * k + 8, :], axis=0, keepdims=True)
        wide_ref[5:6, 0:width] = jnp.sum(skip_acc[...], axis=0, keepdims=True)
        head_ref[...] = jnp.zeros_like(head_ref)
        head_ref[0:1, :] = jnp.sum(head_acc[0:8], axis=0, keepdims=True)
        head_ref[1:2, :] = jnp.sum(head_acc[8:16], axis=0, keepdims=True)


def mixer_backward(perm, slots, vsd, g_mixed, states, taps, shift, bias, rate, skip):
    seq, width = g_mixed.shape
    pairs = width // LANES
    parts = perm.shape[0]
    rows = seq // parts // slots
    subs = rows // CHUNK
    full = width + 2 * LANES
    here = lambda s, i, perm: (perm[parts - 1 - i] * slots + s, 0)

    def halo(s, i, perm):
        before = perm[jnp.maximum(parts - 2 - i, 0)] * slots + s
        return (before * (rows // 8) + rows // 8 - 1, 0)

    return pl.pallas_call(
        functools.partial(backward_kernel, pairs, rows, parts),
        grid_spec=pltpu.PrefetchScalarGridSpec(
            num_scalar_prefetch=1,
            grid=(slots, parts),
            in_specs=[
                row_spec(rows, full + LANES, here),
                row_spec(8, full + LANES, halo),
                row_spec(rows, width, here),
                pl.BlockSpec((subs, LANES, width),
                             lambda s, i, perm: (s * parts + parts - 1 - i, 0, 0)),
                const_spec(taps.shape), const_spec(shift.shape), const_spec(bias.shape),
                const_spec(rate.shape), const_spec(skip.shape),
            ],
            out_specs=[
                row_spec(rows, full + LANES, here),
                const_spec((8, full)),
                const_spec((8, LANES)),
            ],
            scratch_shapes=[
                pltpu.VMEM((8 + rows, full), F32),
                pltpu.VMEM((8 + rows, full), F32),
                pltpu.VMEM((LANES, width), F32),
                pltpu.VMEM((40, full), F32),
                pltpu.VMEM((8, width), F32),
                pltpu.VMEM((16, LANES), F32),
            ],
        ),
        out_shape=[
            jax.ShapeDtypeStruct((seq, full + LANES), BF16),
            jax.ShapeDtypeStruct((8, full), F32),
            jax.ShapeDtypeStruct((8, LANES), F32),
        ],
        cost_estimate=pl.CostEstimate(flops=seq * width * 12000, bytes_accessed=seq * width * 16,
                                      transcendentals=seq * width * 6),
        name="mixer_backward",
    )(perm, vsd, vsd, g_mixed, states, taps, shift, bias, rate, skip)


def hidden_kernel(rows, perm_ref, len_ref, cot_ref, weight_ref, hid_ref, out_ref, dots_ref):
    width = out_ref.shape[1]
    length = len_ref[pl.program_id(0)]
    at = pl.program_id(1) * rows + lax.broadcasted_iota(jnp.int32, (rows, 1), 0)
    grad = dot(cot_ref[...], weight_ref[...])
    for sub in range(rows // CHUNK):
        rs = slice(sub * CHUNK, sub * CHUNK + CHUNK)
        valid = at[rs] < length
        total = jnp.zeros((CHUNK, LANES), F32)
        for tile in range(width // LANES):
            lanes = slice(tile * LANES, tile * LANES + LANES)
            part = jnp.where(valid, grad[rs, lanes], 0.0)
            out_ref[rs, lanes] = part
            total = total + part * hid_ref[rs, lanes].astype(F32)
        dots_ref[8 * sub:8 * sub + 8, :] = dot_nt(jnp.ones((8, LANES), F32), total, HI)


def hidden_grad(perm, slots, lengths, cot, weight, hid):
    seq, width = hid.shape
    depth = cot.shape[1]
    parts = perm.shape[0]
    rows = seq // parts // slots
    subs = rows // CHUNK
    here = lambda s, i, perm, lens: (perm[i] * slots + s, 0)
    return pl.pallas_call(
        functools.partial(hidden_kernel, rows),
        grid_spec=pltpu.PrefetchScalarGridSpec(
            num_scalar_prefetch=2,
            grid=(slots, parts),
            in_specs=[
                row_spec(rows, depth, here),
                pl.BlockSpec(weight.shape, lambda s, i, perm, lens: (0, 0)),
                row_spec(rows, width, here),
            ],
            out_specs=[row_spec(rows, width, here), row_spec(8 * subs, LANES, here)],
        ),
        out_shape=[
            jax.ShapeDtypeStruct((seq, width), F32),
            jax.ShapeDtypeStruct((seq // CHUNK * 8, LANES), F32),
        ],
        cost_estimate=pl.CostEstimate(flops=2 * seq * width * depth,
                                      bytes_accessed=seq * (width * 6 + depth * 2),
                                      transcendentals=0),
        name="hidden_grad",
    )(perm, lengths, cot, weight, hid)


def gate_kernel(rows, inner, perm_ref, len_ref, mixed_ref, gate_ref, gh_ref, sq_ref, dots_ref,
                gain_ref, gm_ref, low_ref, hid_ref, sum_ref, acc):
    width = gm_ref.shape[1]
    length = len_ref[pl.program_id(0)]
    first = jnp.logical_and(pl.program_id(0) == 0, pl.program_id(1) == 0)
    last = jnp.logical_and(pl.program_id(0) == pl.num_programs(0) - 1,
                           pl.program_id(1) == pl.num_programs(1) - 1)

    @pl.when(first)
    def _():
        acc[...] = jnp.zeros_like(acc)

    for sub in range(rows // CHUNK):
        rs = slice(sub * CHUNK, sub * CHUNK + CHUNK)
        at = pl.program_id(1) * rows + sub * CHUNK + iota2(0)
        valid = at < length
        r_row = lax.rsqrt(sq_ref[8 * sub:8 * sub + 1, :] / inner + norm_eps)
        c_row = r_row * r_row * r_row * dots_ref[8 * sub:8 * sub + 1, :] / inner
        r = jnp.broadcast_to(r_row, (CHUNK, LANES)).T
        c = jnp.broadcast_to(c_row, (CHUNK, LANES)).T
        for tile in range(width // LANES):
            lanes = slice(tile * LANES, tile * LANES + LANES)
            mixed = mixed_ref[rs, lanes]
            gate = gate_ref[rs, lanes]
            grad = gh_ref[rs, lanes]
            gain = gain_ref[:, lanes]
            sig = sigmoid(gate)
            act = gate * sig
            gated = mixed * act
            scaled = gated * r
            hid_ref[rs, lanes] = jnp.where(valid, scaled * gain, 0.0).astype(BF16)
            term = grad * scaled
            acc[:, lanes] += sum(term[8 * i:8 * i + 8] for i in range(CHUNK // 8))
            g_gated = r * (grad * gain) - gated * c
            gm_ref[rs, lanes] = g_gated * act
            low_ref[rs, lanes] = (g_gated * mixed * (sig * (1.0 + gate * (1.0 - sig)))).astype(BF16)

    @pl.when(last)
    def _():
        sum_ref[...] = jnp.broadcast_to(jnp.sum(acc[...], axis=0, keepdims=True), sum_ref.shape)


def gate_backward(perm, slots, inner, lengths, mixed, gate_in, g_hidden, sq, dots, gain):
    seq, width = mixed.shape
    parts = perm.shape[0]
    rows = seq // parts // slots
    subs = rows // CHUNK
    here = lambda s, i, perm, lens: (perm[i] * slots + s, 0)
    fixed = lambda s, i, perm, lens: (0, 0)
    return pl.pallas_call(
        functools.partial(gate_kernel, rows, inner),
        grid_spec=pltpu.PrefetchScalarGridSpec(
            num_scalar_prefetch=2,
            grid=(slots, parts),
            in_specs=[
                row_spec(rows, width, here), row_spec(rows, width, here),
                row_spec(rows, width, here), row_spec(8 * subs, LANES, here),
                row_spec(8 * subs, LANES, here), pl.BlockSpec((1, width), fixed),
            ],
            out_specs=[
                row_spec(rows, width, here), row_spec(rows, width, here),
                row_spec(rows, width, here), pl.BlockSpec((8, width), fixed),
            ],
            scratch_shapes=[pltpu.VMEM((8, width), F32)],
        ),
        out_shape=[
            jax.ShapeDtypeStruct((seq, width), F32),
            jax.ShapeDtypeStruct((seq, width), BF16),
            jax.ShapeDtypeStruct((seq, width), BF16),
            jax.ShapeDtypeStruct((8, width), F32),
        ],
        cost_estimate=pl.CostEstimate(flops=seq * width * 200, bytes_accessed=seq * width * 20,
                                      transcendentals=seq * width * 2),
        name="gate_backward",
    )(perm, lengths, mixed, gate_in, g_hidden, sq, dots, gain)


def flip(array, axis, bit):
    size = lax.axis_size(axis)
    return lax.ppermute(array, axis, [(i, i ^ bit) for i in range(size)])


def gather_rows(own):
    pair = jnp.concatenate([own, flip(own, "tensor", 2)], axis=0)
    return jnp.concatenate([pair, flip(pair, "tensor", 1)], axis=0)


def scatter_rows(partial):
    half = partial.shape[0] // 2
    pair = partial[:half].astype(F32) + flip(partial[half:], "tensor", 1).astype(F32)
    quarter = half // 2
    return pair[:quarter] + flip(pair[quarter:].astype(BF16), "tensor", 2).astype(F32)


def sum_rows(array):
    lanes = array.shape[-1]
    split = array.reshape(2, 2, -1, lanes)
    split = split + flip(split, "tensor", 1)[::-1]
    split = split + flip(split, "tensor", 2)[:, ::-1]
    return split.reshape(array.shape)


def sum_over(array, axis):
    bit = 1
    while bit < lax.axis_size(axis):
        array = array + flip(array, axis, bit)
        bit *= 2
    return array


def swap_pieces(pieces, near):
    groups = pieces.shape[0]
    if groups <= 16:
        return jnp.stack([pieces[0]] + [flip(pieces[k], "dp", k) for k in range(1, groups)])
    moved = lax.all_to_all(jnp.take(pieces, near, axis=0), "dp", split_axis=0, concat_axis=0,
                           tiled=True)
    return jnp.take(moved, near, axis=0)


def route(array, origin, group):
    micro, rows, width = array.shape
    groups = lax.axis_size("dp")
    near = group ^ jnp.arange(groups, dtype=jnp.int32)
    pieces = array.reshape(micro, groups, rows // groups, width).transpose(1, 0, 2, 3)
    held = swap_pieces(jnp.take(pieces, near, axis=0), near)
    wanted = near[:, None] * micro + jnp.arange(micro, dtype=jnp.int32)[None, :]
    source = jnp.take(origin, wanted)
    where = ((source // micro) ^ group) * micro + source % micro
    chosen = jnp.take(held.reshape((groups * micro,) + held.shape[2:]), where.reshape(-1), axis=0)
    home = jnp.take(swap_pieces(chosen.reshape(held.shape), near), near, axis=0)
    return home.transpose(1, 0, 2, 3).reshape(micro, rows, width)


def pad_lanes(array):
    return jnp.pad(array, ((0, 0), (0, LANES - array.shape[1])))


def shards(
    tokens,
    cotangent,
    lengths,
    order,
    proj_gate,
    proj_values,
    proj_delta,
    proj_state,
    proj_out,
    pre_gain,
    gate_gain,
    value_conv,
    value_shift,
    state_conv,
    state_shift,
    delta_bias,
    decay_log,
    skip_gain,
):
    micro, rows, width = tokens.shape
    parts = lax.axis_size("tensor")
    part_index = lax.axis_index("tensor")
    group = lax.axis_index("dp")
    own_width = proj_gate.shape[1]
    heads = delta_bias.shape[0]
    states = proj_state.shape[1]
    inner_total = own_width * parts
    near_part = part_index ^ jnp.arange(parts, dtype=jnp.int32)
    perm = (near_part >> 1) | ((near_part & 1) << 1)
    slot_ids = jnp.arange(order.shape[0], dtype=jnp.int32)
    inverse = jnp.sum(jnp.where(order[None, :] == slot_ids[:, None], slot_ids[None, :], 0), axis=1)
    local_slots = group * micro + jnp.arange(micro, dtype=jnp.int32)
    lengths_here = jnp.take(lengths, local_slots)

    delta_pad = jnp.pad(proj_delta, ((0, 0), (0, LANES - heads)))
    own_vsd = jnp.concatenate([proj_values, proj_state, delta_pad], axis=1)
    full_vsd = lax.all_gather(own_vsd, "dp", axis=0, tiled=True)
    full_gate = lax.all_gather(proj_gate, "dp", axis=0, tiled=True)
    full_out = lax.all_gather(proj_out, "dp", axis=0, tiled=True)

    own = tokens.astype(F32)
    scale = lax.rsqrt(jnp.mean(own * own, axis=-1, keepdims=True) + norm_eps)
    normed = (own * scale * pre_gain).astype(BF16).reshape(micro * rows, width)
    all_normed = gather_rows(normed)
    own_cot = route(cotangent, inverse, group)
    all_cot = gather_rows(own_cot.reshape(micro * rows, width))

    taps = jnp.concatenate([value_conv, state_conv], axis=0).T
    shift = jnp.concatenate([value_shift, state_shift])[None, :]
    bias = pad_lanes(delta_bias[None, :])
    rate = pad_lanes(-jnp.exp(decay_log)[None, :])
    skip = jnp.repeat(skip_gain, own_width // heads)[None, :]
    gain = gate_gain[None, :]

    vsd = jnp.dot(all_normed, full_vsd, preferred_element_type=F32)
    gate_in = jnp.dot(all_normed, full_gate, preferred_element_type=F32)
    mixed, hid, sq, kept = mixer_forward(perm, micro, vsd, gate_in, taps, shift, bias, rate, skip,
                                         gain)
    sq = sum_rows(sq)
    partial_out = jnp.einsum("lc,dc->ld", hid, full_out, preferred_element_type=F32)
    branch = scatter_rows(partial_out.astype(BF16)).reshape(micro, rows, width)
    own_chunks = micro * rows // CHUNK
    own_sq = sq[: 8 * own_chunks : 8].reshape(micro, rows, 1)
    own_r = lax.rsqrt(own_sq / inner_total + norm_eps)
    own_pos = part_index * rows + jnp.arange(rows, dtype=jnp.int32)
    valid = (own_pos[None, :] < lengths_here[:, None]).astype(F32)[:, :, None]
    out_here = (own + valid * (branch * own_r)).astype(BF16)
    out_tokens = route(out_here, order, group)

    g_hidden, dots = hidden_grad(perm, micro, lengths_here, all_cot, full_out, hid)
    dots = sum_rows(dots)
    g_mixed, low_gate, hidden, gain_sum = gate_backward(
        perm, micro, inner_total, lengths_here, mixed, gate_in, g_hidden, sq, dots, gain)
    grad_out = jnp.einsum("ld,lc->dc", all_cot, hidden, preferred_element_type=F32).astype(BF16)
    grad_gate = jnp.einsum("ld,lc->dc", all_normed, low_gate,
                           preferred_element_type=F32).astype(BF16)
    grad_out = lax.psum_scatter(grad_out, "dp", scatter_dimension=0, tiled=True)
    grad_gate = lax.psum_scatter(grad_gate, "dp", scatter_dimension=0, tiled=True)

    low_vsd, wide, head = mixer_backward(perm, micro, vsd, g_mixed, kept, taps, shift, bias, rate,
                                         skip)
    grad_vsd = jnp.einsum("ld,lc->dc", all_normed, low_vsd, preferred_element_type=F32).astype(BF16)
    grad_vsd = lax.psum_scatter(grad_vsd, "dp", scatter_dimension=0, tiled=True).astype(F32)
    partial_in = jnp.einsum("lc,dc->ld", low_gate, full_gate, preferred_element_type=F32)
    partial_in = partial_in + jnp.einsum("lc,dc->ld", low_vsd, full_vsd,
                                         preferred_element_type=F32)
    g_normed = scatter_rows(partial_in.astype(BF16)).reshape(micro, rows, width)
    grad_pre = jnp.sum(g_normed * own * scale, axis=(0, 1))
    gained = g_normed * pre_gain
    grad_own = scale * gained - own * scale**3 * jnp.sum(gained * own, axis=-1,
                                                         keepdims=True) / width
    grad_tokens = (own_cot.astype(F32) + grad_own).astype(BF16)

    grad_values = grad_vsd[:, :own_width]
    grad_state = sum_over(grad_vsd[:, own_width:own_width + states], "tensor")
    grad_delta = grad_vsd[:, own_width + states:own_width + states + heads]

    small = jnp.concatenate([wide.reshape(-1, LANES), head[:2], gain_sum[0].reshape(-1, LANES),
                             grad_pre.reshape(-1, LANES)], axis=0)
    small = gather_rows(sum_over(small, "dp")).reshape((parts,) + small.shape)
    small = jnp.take(small, perm, axis=0)
    full = own_width + states
    count = wide.size // LANES
    wides = small[:, :count].reshape(parts, 8, full)
    heads_sum = small[:, count:count + 2]
    gains = small[:, count + 2:count + 2 + own_width // LANES].reshape(parts * own_width)
    pre_sum = jnp.sum(small[:, count + 2 + own_width // LANES:], axis=0).reshape(width)
    state_sum = jnp.sum(wides[:, :5, own_width:], axis=0)
    skip_sum = wides[:, 5, :own_width].reshape(parts * heads, own_width // heads).sum(axis=1)
    return (
        out_tokens,
        grad_tokens,
        grad_gate.astype(F32),
        grad_values,
        grad_delta,
        grad_state,
        grad_out.astype(F32),
        pre_sum,
        gains,
        wides[:, :4, :own_width].transpose(0, 2, 1).reshape(parts * own_width, 4),
        wides[:, 4, :own_width].reshape(parts * own_width),
        state_sum[:4].T,
        state_sum[4],
        heads_sum[:, 0, :heads].reshape(parts * heads),
        heads_sum[:, 1, :heads].reshape(parts * heads),
        skip_sum,
    )


def solution(mesh):
    placed = (
        P("dp", "tensor", None),
        P("dp", "tensor", None),
        P(),
        P(),
        P("dp", "tensor"),
        P("dp", "tensor"),
        P("dp", "tensor"),
        P("dp", None),
        P("dp", "tensor"),
        P(),
        P("tensor"),
        P("tensor", None),
        P("tensor"),
        P(),
        P(),
        P("tensor"),
        P("tensor"),
        P("tensor"),
    )
    return jax.shard_map(
        shards,
        mesh=mesh,
        in_specs=placed,
        out_specs=(
            P("dp", "tensor", None),
            P("dp", "tensor", None),
            P("dp", "tensor"),
            P("dp", "tensor"),
            P("dp", "tensor"),
            P("dp", None),
            P("dp", "tensor"),
            P(),
            P(),
            P(),
            P(),
            P(),
            P(),
            P(),
            P(),
            P(),
        ),
        check_vma=False,
    )
```

```python
import functools
import jax
import jax.numpy as jnp
from jax import lax
from jax.experimental import pallas as pl
from jax.experimental.pallas import tpu as pltpu
from jax.sharding import PartitionSpec as P


LANES = 128
CHUNK = 128
F32 = jnp.float32
BF16 = jnp.bfloat16
HI = lax.Precision.HIGHEST
norm_eps = 1e-05
DP, TP, CLIP = "dp", "tensor", "clip"
ROWS = "ld,lc->dc"
LOG2E = 1.4426950408889634


def dot(a, b, precision=None):
    return lax.dot_general(a, b, (((1,), (0,)), ((), ())), precision=precision,
                           preferred_element_type=F32)


def dot_nt(a, b, precision=None):
    return lax.dot_general(a, b, (((1,), (1,)), ((), ())), precision=precision,
                           preferred_element_type=F32)


def iota2(axis):
    return lax.broadcasted_iota(jnp.int32, (CHUNK, LANES), axis)


def conv_tile(buf, tile, row, taps_ref, shift_ref):
    lanes = slice(tile * LANES, tile * LANES + LANES)
    total = jnp.broadcast_to(shift_ref[:, lanes], (CHUNK, LANES))
    for k in range(4):
        total = total + taps_ref[k:k + 1, lanes] * buf[tile, row + 5 + k:row + 5 + k + CHUNK, :]
    return total


def sigmoid(v):
    return 0.5 * jnp.tanh(0.5 * v) + 0.5


def softplus(v):
    return jnp.maximum(v, 0.0) + jnp.log(1.0 + jnp.exp(-jnp.abs(v)))


def fold(v):
    return sum(v[8 * i:8 * i + 8] for i in range(v.shape[0] // 8))


def spread_heads(spread_ref, *rows):
    rows = jnp.concatenate(rows, axis=0)
    high = rows.astype(BF16)
    low = (rows - high.astype(F32)).astype(BF16)
    return dot(jnp.concatenate([high, low], axis=1), spread_ref[...])


def decays(delta_in, bias_ref, rate_ref, lower):
    v = delta_in + bias_ref[...]
    delta = softplus(v)
    a = delta * rate_ref[...]
    cum = dot(lower.astype(F32), a, HI) * LOG2E
    last = cum[CHUNK - 1:CHUNK, :]
    return v, delta, a, cum, jnp.exp2(cum), jnp.exp2(last - cum), jnp.exp2(last)


def halves(v, low_half):
    return jnp.concatenate([jnp.where(low_half, v, 0.0), jnp.where(low_half, 0.0, v)], axis=0)


def forward_kernel(pairs, rows, perm_ref, vsd_ref, gate_ref, taps_ref, shift_ref, bias_ref,
                   rate_ref, skip_ref, gain_ref, spread_ref, mixed_ref, hid_ref, sq_ref, st_ref, buf,
                   state, wide):
    width = pairs * LANES
    tiles = pairs + 2
    step = pl.program_id(1)

    @pl.when(step == 0)
    def _():
        buf[:, 0:8, :] = jnp.zeros((tiles, 8, LANES), F32)
        state[...] = jnp.zeros_like(state)

    for tile in range(tiles):
        buf[tile, 8:8 + rows, :] = vsd_ref[:, tile * LANES:tile * LANES + LANES]
    row_i, col_j = iota2(0), iota2(1)
    lower = row_i >= col_j
    low_half = col_j < LANES // 2
    for sub in range(rows // CHUNK):
        r0 = sub * CHUNK
        rs = slice(r0, r0 + CHUNK)
        pre_b = conv_tile(buf, pairs, r0, taps_ref, shift_ref)
        pre_c = conv_tile(buf, pairs + 1, r0, taps_ref, shift_ref)
        b_act = pre_b * sigmoid(pre_b)
        c_low = (pre_c * sigmoid(pre_c)).astype(BF16)
        b_low = b_act.astype(BF16)
        b_t = b_act.T.astype(BF16)
        _, delta, _, cum, eq, te, _ = decays(
            vsd_ref[rs, width + 2 * LANES:width + 3 * LANES], bias_ref, rate_ref, lower)
        cum_t = cum.T
        wide[...] = spread_heads(spread_ref, delta, eq, te)
        cb = dot_nt(c_low, b_low)
        squares = jnp.zeros((CHUNK, LANES), F32)
        for hp in range(pairs):
            lanes = slice(hp * LANES, hp * LANES + LANES)
            pre = conv_tile(buf, hp, r0, taps_ref, shift_ref)
            x = pre * sigmoid(pre)
            xw = x * wide[0:CHUNK, lanes]
            xw_low = xw.astype(BF16)
            inner = []
            for h in (2 * hp, 2 * hp + 1):
                gap = jnp.where(lower, cum[:, h:h + 1] - cum_t[h:h + 1, :], -10000.0)
                inner.append(dot((cb * jnp.exp2(gap)).astype(BF16), xw_low))
            st = state[:, lanes]
            st_low = st.astype(BF16)
            st_ref[sub, :, lanes] = st_low
            y = (jnp.where(low_half, inner[0], inner[1])
                 + dot(c_low, st_low) * wide[CHUNK:2 * CHUNK, lanes] + skip_ref[:, lanes] * x)
            state[:, lanes] = (st * wide[2 * CHUNK - 1:2 * CHUNK, lanes]
                               + dot(b_t, (xw * wide[2 * CHUNK:3 * CHUNK, lanes]).astype(BF16)))
            mixed_ref[rs, lanes] = y.astype(mixed_ref.dtype)
            gate = gate_ref[rs, lanes].astype(F32)
            gated = y * (gate * sigmoid(gate))
            hid_ref[rs, lanes] = (gated * gain_ref[:, lanes]).astype(BF16)
            squares = squares + gated * gated
        sq_ref[8 * sub:8 * sub + 8, :] = dot_nt(jnp.ones((8, LANES), F32), squares, HI)
    for tile in range(tiles):
        buf[tile, 0:8, :] = buf[tile, rows:rows + 8, :]


def row_spec(rows, width, where):
    return pl.BlockSpec((rows, width), where)


def const_spec(shape):
    return pl.BlockSpec(shape, lambda s, i, perm: (0,) * len(shape))


def mixer_forward(perm, slots, vsd, gate_in, taps, shift, bias, rate, skip, gain, spread):
    seq, width = gate_in.shape
    pairs = width // LANES
    parts = perm.shape[0]
    rows = seq // parts // slots
    subs = rows // CHUNK
    here = lambda s, i, perm: (perm[i] * slots + s, 0)
    return pl.pallas_call(
        functools.partial(forward_kernel, pairs, rows),
        grid_spec=pltpu.PrefetchScalarGridSpec(
            num_scalar_prefetch=1,
            grid=(slots, parts),
            in_specs=[
                row_spec(rows, width + 3 * LANES, here),
                row_spec(rows, width, here),
                const_spec(taps.shape), const_spec(shift.shape), const_spec(bias.shape),
                const_spec(rate.shape), const_spec(skip.shape), const_spec(gain.shape),
                const_spec(spread.shape),
            ],
            out_specs=[
                row_spec(rows, width, here),
                row_spec(rows, width, here),
                row_spec(8 * subs, LANES, here),
                pl.BlockSpec((subs, LANES, width), lambda s, i, perm: (s * parts + i, 0, 0)),
            ],
            scratch_shapes=[
                pltpu.VMEM((pairs + 2, 8 + rows, LANES), F32),
                pltpu.VMEM((LANES, width), F32),
                pltpu.VMEM((3 * CHUNK, width), F32),
            ],
        ),
        out_shape=[
            jax.ShapeDtypeStruct((seq, width), BF16),
            jax.ShapeDtypeStruct((seq, width), BF16),
            jax.ShapeDtypeStruct((seq // CHUNK * 8, LANES), F32),
            jax.ShapeDtypeStruct((seq // CHUNK, LANES, width), BF16),
        ],
        cost_estimate=pl.CostEstimate(flops=seq * width * 6000, bytes_accessed=seq * width * 16,
                                      transcendentals=seq * width * 4),
        name="mixer_forward",
    )(perm, vsd, gate_in, taps, shift, bias, rate, skip, gain, spread)


def backward_kernel(pairs, rows, parts, perm_ref, vsd_ref, halo_ref, gm_ref, st_ref, taps_ref,
                    shift_ref, bias_ref, rate_ref, skip_ref, place_ref, spread_ref, low_ref, wide_ref, head_ref,
                    buf, gbuf, dstate, taps_acc, skip_acc, head_acc, terms, g_eqs, xw_tes, lane):
    width = pairs * LANES
    full = width + 2 * LANES
    tiles = pairs + 2
    step = pl.program_id(1)
    first = jnp.logical_and(step == 0, pl.program_id(0) == 0)
    last = jnp.logical_and(step == parts - 1, pl.program_id(0) == pl.num_programs(0) - 1)
    subs = rows // CHUNK

    @pl.when(step == 0)
    def _():
        gbuf[:, rows:rows + 8, :] = jnp.zeros((tiles, 8, LANES), F32)
        dstate[...] = jnp.zeros_like(dstate)

    @pl.when(first)
    def _():
        taps_acc[...] = jnp.zeros_like(taps_acc)
        skip_acc[...] = jnp.zeros_like(skip_acc)
        head_acc[...] = jnp.zeros_like(head_acc)

    for tile in range(tiles):
        lanes = slice(tile * LANES, tile * LANES + LANES)
        buf[tile, 8:8 + rows, :] = vsd_ref[:, lanes]
        buf[tile, 0:8, :] = jnp.where(step == parts - 1, 0.0, halo_ref[:, lanes])
    row_i, col_j = iota2(0), iota2(1)
    lower = row_i >= col_j
    upper = col_j >= row_i
    strict = row_i > col_j
    low_half = col_j < LANES // 2
    row_8 = lax.broadcasted_iota(jnp.int32, (8, LANES), 0)
    for sub in reversed(range(subs)):
        r0 = sub * CHUNK
        rs = slice(r0, r0 + CHUNK)
        pre_b = conv_tile(buf, pairs, r0, taps_ref, shift_ref)
        pre_c = conv_tile(buf, pairs + 1, r0, taps_ref, shift_ref)
        sig_b = sigmoid(pre_b)
        sig_c = sigmoid(pre_c)
        b_low = (pre_b * sig_b).astype(BF16)
        c_act = pre_c * sig_c
        c_low = c_act.astype(BF16)
        c_t = c_act.T.astype(BF16)
        v, delta, a, cum, eq, te, eq_last = decays(
            vsd_ref[rs, full:full + LANES], bias_ref, rate_ref, lower)
        cum_t = cum.T
        lane[...] = spread_heads(spread_ref, delta, eq, te)
        bc = dot_nt(b_low, c_low)
        d_bc = jnp.zeros((CHUNK, LANES), F32)
        col_sum = jnp.zeros((CHUNK, LANES), F32)
        row_sums = [jnp.zeros((8, LANES), F32)] * (-(-2 * pairs // 8))
        for hp in range(pairs):
            lanes = slice(hp * LANES, hp * LANES + LANES)
            pre = conv_tile(buf, hp, r0, taps_ref, shift_ref)
            sig = sigmoid(pre)
            x = pre * sig
            d_lane = lane[0:CHUNK, lanes]
            te_lane = lane[2 * CHUNK:3 * CHUNK, lanes]
            xw = x * d_lane
            g_low = gm_ref[rs, lanes]
            g = g_low.astype(F32)
            d_mix = dot_nt(halves(xw.astype(BF16), low_half), g_low)
            inner = []
            for side, h in enumerate((2 * hp, 2 * hp + 1)):
                gap = jnp.where(upper, cum_t[h:h + 1, :] - cum[:, h:h + 1], -10000.0)
                e = jnp.exp2(gap)
                m = bc * e
                inner.append(dot(m.astype(BF16), g_low))
                d_m = d_mix[side * CHUNK:side * CHUNK + CHUNK, :]
                d_bc = d_bc + d_m * e
                p = d_m * m
                col_sum = jnp.where(col_j == h, jnp.sum(p, axis=1, keepdims=True), col_sum)
                row_sums[h // 8] = jnp.where(row_8 == h % 8, jnp.sum(p, axis=0, keepdims=True),
                                             row_sums[h // 8])
            st = st_ref[sub, :, lanes]
            ds = dstate[:, lanes]
            ds_low = ds.astype(BF16)
            g_eq = g * lane[CHUNK:2 * CHUNK, lanes]
            g_eq_low = g_eq.astype(BF16)
            xw_te = xw * te_lane
            b_ds = dot(b_low, ds_low)
            d_xw = jnp.where(low_half, inner[0], inner[1]) + te_lane * b_ds
            terms[0:CHUNK, lanes] = (g_eq * dot(c_low, st)).astype(BF16)
            terms[CHUNK:2 * CHUNK, lanes] = (xw_te * b_ds).astype(BF16)
            terms[2 * CHUNK:3 * CHUNK, lanes] = (x * d_xw).astype(BF16)
            terms[3 * CHUNK:3 * CHUNK + 16, lanes] = jnp.concatenate(
                [fold(ds * st.astype(F32)), jnp.zeros((8, LANES), F32)], axis=0).astype(BF16)
            g_eqs[:, lanes] = g_eq_low
            xw_tes[:, lanes] = xw_te.astype(BF16)
            g_x = d_lane * d_xw + skip_ref[:, lanes] * g
            skip_acc[:, lanes] += fold(g * x)
            gbuf[hp, rs, :] = g_x * (sig * (1.0 + pre * (1.0 - sig)))
        sums = dot(terms[...], place_ref[...])
        d_low = dstate[...].astype(BF16)
        g_b = dot_nt(xw_tes[...], d_low) + dot(d_bc.astype(BF16), c_low)
        g_c = dot_nt(g_eqs[...], st_ref[sub]) + dot(d_bc.T.astype(BF16), b_low)
        for hp in range(pairs):
            lanes = slice(hp * LANES, hp * LANES + LANES)
            dstate[:, lanes] = (dstate[:, lanes] * lane[2 * CHUNK - 1:2 * CHUNK, lanes]
                                + dot(c_t, g_eqs[:, lanes]))
        gbuf[pairs, rs, :] = g_b * (sig_b * (1.0 + pre_b * (1.0 - sig_b)))
        gbuf[pairs + 1, rs, :] = g_c * (sig_c * (1.0 + pre_c * (1.0 - sig_c)))
        row_sum = jnp.concatenate(
            row_sums + [jnp.zeros((CHUNK - 8 * len(row_sums), LANES), F32)], axis=0).T
        g_cum = row_sum - col_sum + sums[0:CHUNK]
        inner = jnp.sum(sums[3 * CHUNK:3 * CHUNK + 8], axis=0, keepdims=True)
        g_a = (dot(upper.astype(F32), g_cum, HI) + dot(strict.astype(F32), sums[CHUNK:2 * CHUNK], HI)
               + eq_last * inner)
        g_delta = sums[2 * CHUNK:3 * CHUNK] + rate_ref[...] * g_a
        g_din = g_delta * sigmoid(v)
        low_ref[rs, full:full + LANES] = g_din.astype(BF16)
        head_acc[0:8] += fold(g_din)
        head_acc[8:16] += fold(a * g_a)
    for tile in range(tiles):
        lanes = slice(tile * LANES, tile * LANES + LANES)
        for sub in range(subs):
            r0 = sub * CHUNK
            g_in = jnp.zeros((CHUNK, LANES), F32)
            g_pre = gbuf[tile, r0:r0 + CHUNK, :]
            for k in range(4):
                g_in = g_in + (taps_ref[k:k + 1, lanes]
                               * gbuf[tile, r0 + 3 - k:r0 + 3 - k + CHUNK, :])
                taps_acc[8 * k:8 * k + 8, lanes] += fold(
                    g_pre * buf[tile, r0 + 5 + k:r0 + 5 + k + CHUNK, :])
            taps_acc[32:40, lanes] += fold(g_pre)
            low_ref[r0:r0 + CHUNK, lanes] = g_in.astype(BF16)
        gbuf[tile, rows:rows + 8, :] = gbuf[tile, 0:8, :]

    @pl.when(last)
    def _():
        wide_ref[...] = jnp.zeros_like(wide_ref)
        for k in range(5):
            wide_ref[k:k + 1, :] = jnp.sum(taps_acc[8 * k:8 * k + 8, :], axis=0, keepdims=True)
        wide_ref[5:6, 0:width] = jnp.sum(skip_acc[...], axis=0, keepdims=True)
        head_ref[...] = jnp.zeros_like(head_ref)
        head_ref[0:1, :] = jnp.sum(head_acc[0:8], axis=0, keepdims=True)
        head_ref[1:2, :] = jnp.sum(head_acc[8:16], axis=0, keepdims=True)


def mixer_backward(perm, slots, slot, vsd, g_mixed, states, taps, shift, bias, rate, skip, place,
                   spread, low):
    seq, width = g_mixed.shape
    pairs = width // LANES
    parts = perm.shape[0]
    rows = seq // parts // slots
    subs = rows // CHUNK
    full = width + 2 * LANES
    here = lambda s, i, perm: (perm[parts - 1 - i] * slots + slot, 0)
    inputs = 12

    def halo(s, i, perm):
        before = perm[jnp.maximum(parts - 2 - i, 0)] * slots + slot
        return (before * (rows // 8) + rows // 8 - 1, 0)

    def body(*refs):
        backward_kernel(pairs, rows, parts, *(refs[:inputs] + refs[len(refs) - 13:]))

    kept = () if low is None else (low,)
    return pl.pallas_call(
        body,
        grid_spec=pltpu.PrefetchScalarGridSpec(
            num_scalar_prefetch=1,
            grid=(1, parts),
            in_specs=[
                row_spec(rows, full + LANES, here),
                row_spec(8, full + LANES, halo),
                row_spec(rows, width, here),
                pl.BlockSpec((subs, LANES, width),
                             lambda s, i, perm: (slot * parts + parts - 1 - i, 0, 0)),
                const_spec(taps.shape), const_spec(shift.shape), const_spec(bias.shape),
                const_spec(rate.shape), const_spec(skip.shape), const_spec(place.shape),
                const_spec(spread.shape),
            ] + [pl.BlockSpec(memory_space=pl.ANY)] * len(kept),
            out_specs=[
                row_spec(rows, full + LANES, here),
                const_spec((8, full)),
                const_spec((8, LANES)),
            ],
            scratch_shapes=[
                pltpu.VMEM((pairs + 2, 8 + rows, LANES), F32),
                pltpu.VMEM((pairs + 2, 8 + rows, LANES), F32),
                pltpu.VMEM((LANES, width), F32),
                pltpu.VMEM((40, full), F32),
                pltpu.VMEM((8, width), F32),
                pltpu.VMEM((16, LANES), F32),
                pltpu.VMEM((3 * CHUNK + 16, width), BF16),
                pltpu.VMEM((CHUNK, width), BF16),
                pltpu.VMEM((CHUNK, width), BF16),
                pltpu.VMEM((3 * CHUNK, width), F32),
            ],
        ),
        out_shape=[
            jax.ShapeDtypeStruct((seq, full + LANES), BF16),
            jax.ShapeDtypeStruct((8, full), F32),
            jax.ShapeDtypeStruct((8, LANES), F32),
        ],
        input_output_aliases={inputs: 0} if kept else {},
        cost_estimate=pl.CostEstimate(flops=seq // slots * width * 12000,
                                      bytes_accessed=seq // slots * width * 16,
                                      transcendentals=seq // slots * width * 6),
        name="mixer_backward",
    )(perm, vsd, vsd, g_mixed, states, taps, shift, bias, rate, skip, place, spread, *kept)


def piece_spec(k, quarter, rows, depth):
    return pl.BlockSpec((rows, depth),
                        lambda i, *_: (jnp.clip(i - k * quarter, 0, quarter - 1), 0))


def project_kernel(count, where_ref, *refs):
    shares, pieces = refs[:count], refs[count:count + 4]
    vsd_ref, gate_ref, rows_ref, in_ref, out_ref = refs[count + 4:]
    block = pl.program_id(0)
    vsd_width = vsd_ref.shape[1]
    split = in_ref.shape[1]

    @pl.when(block == 0)
    def _():
        for k, share in enumerate(shares):
            at = pl.ds(pl.multiple_of(where_ref[k], share.shape[0]), share.shape[0])
            in_ref[at, :] = share[:, :split]
            out_ref[at, :] = share[:, split:]

    for k, piece in enumerate(pieces):
        @pl.when(block == k)
        def _(piece=piece):
            rows_ref[...] = piece[...]

    tile = 3 * LANES
    for at in range(0, vsd_width, tile):
        vsd_ref[:, at:at + tile] = dot(rows_ref[...], in_ref[:, at:at + tile])
    for at in range(0, gate_ref.shape[1], tile):
        gate_ref[:, at:at + tile] = dot(
            rows_ref[...], in_ref[:, vsd_width + at:vsd_width + at + tile]).astype(BF16)


def project(pieces, shares, where, split, vsd_width):
    rows, depth = pieces[0].shape
    seq = 4 * rows
    here = lambda i, where: (i, 0)
    fixed = lambda i, where: (0, 0)
    last = shares[0].shape[1] - split
    single = dict(pipeline_mode=pl.Buffered(1))
    return pl.pallas_call(
        functools.partial(project_kernel, len(shares)),
        grid_spec=pltpu.PrefetchScalarGridSpec(
            num_scalar_prefetch=1,
            grid=(4,),
            in_specs=[pl.BlockSpec(share.shape, fixed, **single) for share in shares]
            + [piece_spec(k, 1, rows, depth) for k in range(4)],
            out_specs=[
                pl.BlockSpec((rows, vsd_width), here),
                pl.BlockSpec((rows, split - vsd_width), here),
                pl.BlockSpec((rows, depth), here),
                pl.BlockSpec((depth, split), fixed),
                pl.BlockSpec((depth, last), fixed),
            ],
        ),
        out_shape=[
            jax.ShapeDtypeStruct((seq, vsd_width), F32),
            jax.ShapeDtypeStruct((seq, split - vsd_width), BF16),
            jax.ShapeDtypeStruct((seq, depth), BF16),
            jax.ShapeDtypeStruct((depth, split), BF16),
            jax.ShapeDtypeStruct((depth, last), BF16),
        ],
        cost_estimate=pl.CostEstimate(flops=2 * seq * split * depth, transcendentals=0,
                                      bytes_accessed=seq * (split * 4 + depth * 4)),
        name="project",
    )(where, *shares, *pieces)


def hidden_kernel(rows, slots, part_ref, len_ref, *refs):
    pieces, (weight_ref, hid_ref, out_ref, dots_ref, rows_ref) = refs[:4], refs[4:]
    width = out_ref.shape[1]
    block = pl.program_id(0)
    first_row = part_ref[block] * rows

    for k, piece in enumerate(pieces):
        @pl.when(block == k)
        def _(piece=piece):
            rows_ref[...] = piece[...]

    totals = [jnp.zeros((rows, LANES), F32)] * slots
    tile = 2 * LANES
    at_row = first_row + lax.broadcasted_iota(jnp.int32, (rows, 1), 0)
    for at in range(0, width, tile):
        whole = dot(rows_ref[...], weight_ref[:, at:at + tile])
        for slot in range(slots):
            rs = slice(slot * rows, slot * rows + rows)
            grad = jnp.where(at_row < len_ref[slot], whole[rs], 0.0)
            out_ref[rs, at:at + tile] = grad.astype(BF16)
            for half in range(at, at + tile, LANES):
                totals[slot] = totals[slot] + (grad[:, half - at:half - at + LANES]
                                               * hid_ref[rs, half:half + LANES].astype(F32))
    chunks = rows // CHUNK
    for slot in range(slots):
        for sub in range(chunks):
            at = 8 * (slot * chunks + sub)
            dots_ref[at:at + 8, :] = dot_nt(
                jnp.ones((8, LANES), F32), totals[slot][sub * CHUNK:sub * CHUNK + CHUNK], HI)


def hidden_grad(part_of, slots, lengths, pieces, weight, hid):
    seq, width = hid.shape
    piece_rows, depth = pieces[0].shape
    here = lambda i, inv, lens: (i, 0)
    return pl.pallas_call(
        functools.partial(hidden_kernel, piece_rows // slots, slots),
        grid_spec=pltpu.PrefetchScalarGridSpec(
            num_scalar_prefetch=2,
            grid=(4,),
            in_specs=[
                *(piece_spec(k, 1, piece_rows, depth) for k in range(4)),
                pl.BlockSpec(weight.shape, lambda i, inv, lens: (0, 0),
                             pipeline_mode=pl.Buffered(1)),
                row_spec(piece_rows, width, here),
            ],
            out_specs=[row_spec(piece_rows, width, here),
                       row_spec(piece_rows // CHUNK * 8, LANES, here),
                       row_spec(piece_rows, depth, here)],
        ),
        out_shape=[
            jax.ShapeDtypeStruct((seq, width), BF16),
            jax.ShapeDtypeStruct((seq // CHUNK * 8, LANES), F32),
            jax.ShapeDtypeStruct((seq, depth), BF16),
        ],
        cost_estimate=pl.CostEstimate(flops=2 * seq * width * depth,
                                      bytes_accessed=seq * (width * 6 + depth * 4),
                                      transcendentals=0),
        name="hidden_grad",
    )(part_of, lengths, *pieces, weight, hid)


def gate_kernel(rows, slots, inner, part_ref, len_ref, mixed_ref, gate_ref, gh_ref, stats_ref,
                gain_ref, gm_ref, low_ref, hid_ref, sum_ref, acc):
    width = gm_ref.shape[1]
    block = pl.program_id(0)
    chunks = rows // CHUNK

    @pl.when(block == 0)
    def _():
        acc[...] = jnp.zeros_like(acc)

    for piece in range(slots * chunks):
        rs = slice(piece * CHUNK, piece * CHUNK + CHUNK)
        at = part_ref[block] * rows + (piece % chunks) * CHUNK + iota2(0)
        valid = at < len_ref[piece // chunks]
        row = pl.ds(block * slots * chunks + piece, 1)
        r_row = lax.rsqrt(stats_ref[0, row, :] / inner + norm_eps)
        c_row = r_row * r_row * r_row * stats_ref[1, row, :] / inner
        r = jnp.broadcast_to(r_row, (CHUNK, LANES)).T
        c = jnp.broadcast_to(c_row, (CHUNK, LANES)).T
        for tile in range(width // LANES):
            lanes = slice(tile * LANES, tile * LANES + LANES)
            mixed = mixed_ref[rs, lanes].astype(F32)
            gate = gate_ref[rs, lanes].astype(F32)
            grad = gh_ref[rs, lanes].astype(F32)
            gain = gain_ref[:, lanes]
            sig = sigmoid(gate)
            act = gate * sig
            gated = mixed * act
            scaled = gated * r
            hid_ref[rs, lanes] = jnp.where(valid, scaled * gain, 0.0).astype(BF16)
            acc[:, lanes] += fold(grad * scaled)
            g_gated = r * (grad * gain) - gated * c
            gm_ref[rs, lanes] = (g_gated * act).astype(BF16)
            low_ref[rs, lanes] = (g_gated * mixed * (sig * (1.0 + gate * (1.0 - sig)))).astype(BF16)

    @pl.when(block == pl.num_programs(0) - 1)
    def _():
        sum_ref[...] = jnp.broadcast_to(jnp.sum(acc[...], axis=0, keepdims=True), sum_ref.shape)


def gate_backward(part_of, slots, inner, lengths, mixed, gate_in, g_hidden, stats, gain):
    seq, width = mixed.shape
    rows = seq // 4
    here = pl.BlockSpec((rows, width), lambda i, part, lens: (i, 0))
    fixed = lambda shape: pl.BlockSpec(shape, lambda i, part, lens: (0,) * len(shape))
    return pl.pallas_call(
        functools.partial(gate_kernel, rows // slots, slots, inner),
        grid_spec=pltpu.PrefetchScalarGridSpec(
            num_scalar_prefetch=2,
            grid=(4,),
            in_specs=[here, here, here, fixed(stats.shape), fixed((1, width))],
            out_specs=[here, here, here, fixed((8, width))],
            scratch_shapes=[pltpu.VMEM((8, width), F32)],
        ),
        out_shape=[
            jax.ShapeDtypeStruct((seq, width), BF16),
            jax.ShapeDtypeStruct((seq, width), BF16),
            jax.ShapeDtypeStruct((seq, width), BF16),
            jax.ShapeDtypeStruct((8, width), F32),
        ],
        cost_estimate=pl.CostEstimate(flops=seq * width * 200, bytes_accessed=seq * width * 12,
                                      transcendentals=seq * width * 2),
        name="gate_backward",
    )(part_of, lengths, mixed, gate_in, g_hidden, stats, gain)


def input_kernel(vsd_width, vsd_0, vsd_1, gate_0, gate_1, rows_0, rows_1, weight_ref, away_ref,
                 home_ref, sum_ref):
    depth = weight_ref.shape[0]
    tile = 2 * LANES
    half = rows_0.shape[0]
    vsd = jnp.concatenate([vsd_0[...], vsd_1[...]], axis=0)
    gate = jnp.concatenate([gate_0[...], gate_1[...]], axis=0)

    def write(out_ref, first):
        for at in range(0, depth, tile):
            total = dot_nt(vsd, weight_ref[at:at + tile, :vsd_width])
            total = total + dot_nt(gate, weight_ref[at:at + tile, vsd_width:])
            out_ref[:, at:at + tile] = total.astype(BF16)
            term = (fold(total[:half] * rows_0[:, at:at + tile].astype(F32))
                    + fold(total[half:] * rows_1[:, at:at + tile].astype(F32)))
            sum_ref[:, at:at + tile] = term if first else sum_ref[:, at:at + tile] + term

    @pl.when(pl.program_id(0) == 0)
    def _():
        write(away_ref, True)

    @pl.when(pl.program_id(0) == 1)
    def _():
        write(home_ref, False)


def input_grad(slots, slot, low_vsd, low_gate, normed, weight):
    seq, vsd_width = low_vsd.shape
    depth = weight.shape[0]
    rows = seq // 4 // slots
    here = lambda side: lambda i: ((2 - 2 * i + side) * slots + slot, 0)
    out = jax.ShapeDtypeStruct((2 * rows, depth), BF16)
    whole = lambda height: pl.BlockSpec((height, depth), lambda i: (0, 0))
    pair = lambda width: [pl.BlockSpec((rows, width), here(0)), pl.BlockSpec((rows, width), here(1))]
    return pl.pallas_call(
        functools.partial(input_kernel, vsd_width),
        grid=(2,),
        in_specs=[
            *pair(vsd_width), *pair(low_gate.shape[1]), *pair(depth),
            pl.BlockSpec(weight.shape, lambda i: (0, 0), pipeline_mode=pl.Buffered(1)),
        ],
        out_specs=[whole(2 * rows), whole(2 * rows), whole(8)],
        out_shape=[out, out, jax.ShapeDtypeStruct((8, depth), F32)],
        cost_estimate=pl.CostEstimate(flops=2 * 4 * rows * depth * weight.shape[1],
                                      transcendentals=0, bytes_accessed=weight.size * 2),
        compiler_params=pltpu.CompilerParams(
            vmem_limit_bytes=30 << 20 if slot == slots - 1 else None),
        name="input_grad",
    )(low_vsd, low_vsd, low_gate, low_gate, normed, normed, weight)


def branch_kernel(hid_ref, weight_ref, away_ref, home_ref):
    depth = weight_ref.shape[0]
    tile = 2 * LANES

    def write(out_ref):
        for at in range(0, depth, tile):
            out_ref[:, at:at + tile] = dot_nt(hid_ref[...], weight_ref[at:at + tile, :]).astype(BF16)

    @pl.when(pl.program_id(0) < 2)
    def _():
        write(away_ref)

    @pl.when(pl.program_id(0) >= 2)
    def _():
        write(home_ref)


def branch_rows(hid, weight):
    seq, width = hid.shape
    depth = weight.shape[0]
    rows = seq // 4
    out = jax.ShapeDtypeStruct((2 * rows, depth), BF16)
    return pl.pallas_call(
        branch_kernel,
        grid=(4,),
        in_specs=[
            pl.BlockSpec((rows, width), lambda i: (i ^ 2, 0)),
            pl.BlockSpec(weight.shape, lambda i: (0, 0), pipeline_mode=pl.Buffered(1)),
        ],
        out_specs=[
            pl.BlockSpec((rows, depth), lambda i: (jnp.minimum(i, 1), 0)),
            pl.BlockSpec((rows, depth), lambda i: (jnp.maximum(i - 2, 0), 0)),
        ],
        out_shape=[out, out],
        cost_estimate=pl.CostEstimate(flops=2 * seq * depth * width, transcendentals=0,
                                      bytes_accessed=seq * (width + depth) * 2),
        name="branch_rows",
    )(hid, weight)


def flip(array, axis, bit):
    size = lax.axis_size(axis)
    return lax.ppermute(array, axis, [(i, i ^ bit) for i in range(size)])


def gather_rows(own, direct=False):
    side = flip(own, TP, 1)
    near = flip(own, TP, 2)
    return own, near, side, flip(own, TP, 3) if direct else flip(near, TP, 1)


def scatter_rows(away, home, slots, *behind):
    got = flip(away, TP, 1)
    home = lax.optimization_barrier(home)
    if behind:
        got = after(got, *behind)
    rows = home.shape[0] // 2 // slots
    total = []
    for slot in range(slots):
        near = slice(slot * rows, slot * rows + rows)
        far = slice((slots + slot) * rows, (slots + slot + 1) * rows)
        low = (home[far].astype(F32) + got[far].astype(F32)).astype(BF16)
        total.append((home[near], got[near], flip(low, TP, 2), low))
    return total


def add_terms(terms, *behind):
    home, got, far = terms[:3]
    if behind:
        far = after(far, *behind)
    return home.astype(F32) + got.astype(F32) + far.astype(F32)


def after(value, *others):
    return lax.optimization_barrier((value,) + others)[0]


def sum_rows(stats):
    kinds, _, lanes = stats.shape
    split = stats.reshape(kinds, 2, 2, -1, lanes)
    split = split + flip(split, TP, 1)[:, ::-1]
    split = split + flip(split, TP, 2)[:, :, ::-1]
    return split.reshape(stats.shape)


def sum_over(array, axis):
    bit = 1
    while bit < lax.axis_size(axis):
        array = array + flip(array, axis, bit)
        bit *= 2
    return array


RING = (0, 2, 4, 6, 7, 5, 3, 1)


def ring_pieces(shard, group, ready, late):
    groups = lax.axis_size(DP)
    rows, _ = shard.shape
    half = rows // 2
    ahead = [(RING[i], RING[(i + 1) % groups]) for i in range(groups)]
    back = [(there, here) for here, there in ahead]
    ring = jnp.array(RING, jnp.int32)
    spot = jnp.sum(jnp.where(ring == group, jnp.arange(groups, dtype=jnp.int32), 0))
    steps = jnp.arange(groups, dtype=jnp.int32)
    where = jnp.concatenate([jnp.take(ring, (spot - steps) % groups, mode=CLIP) * rows,
                             jnp.take(ring, (spot + steps) % groups, mode=CLIP) * rows + half])
    up, down = [shard[:half]], [shard[half:]]
    for step in range(groups - 1):
        if step == 3:
            up[-1] = after(up[-1], where, *ready)
        if step == 6:
            up[-1] = after(up[-1], *late)
        up.append(lax.ppermute(up[-1], DP, ahead))
        down.append(lax.ppermute(down[-1], DP, back))
    return up + down, where


def first_half_kernel(axes, where_ref, *refs):
    count = len(axes)
    views, gots, homes, aways = (refs[i * count:i * count + count] for i in range(4))
    for axis, view_ref, got_ref, home_ref, away_ref in zip(axes, views, gots, homes, aways):
        other = where_ref[1] if axis == 2 else where_ref[0]
        for far in range(2):
            for away in range(2):
                near = other ^ away
                mine = view_ref[far, near, 0] if axis == 2 else view_ref[far, 0, near]
                total = mine.astype(F32) + got_ref[far, near].astype(F32)
                if away:
                    away_ref[far] = total.astype(BF16)
                else:
                    home_ref[far] = total


def second_half_kernel(where_ref, *refs):
    count = len(refs) // 4
    homes, gots, owns, aways = (refs[i * count:i * count + count] for i in range(4))
    for home_ref, got_ref, own_ref, away_ref in zip(homes, gots, owns, aways):
        for away in range(2):
            far = where_ref[2] ^ away
            total = home_ref[far] + got_ref[far].astype(F32)
            if away:
                away_ref[...] = total.astype(BF16)
            else:
                own_ref[...] = total


def halve(kernel, where, ins, in_specs, shapes):
    fixed = lambda shape: pl.BlockSpec(shape, lambda i, where: (0,) * len(shape))
    outs = [jax.ShapeDtypeStruct(shape, kind) for kind in (F32, BF16) for shape in shapes]
    size = sum(out.size for out in outs)
    got = pl.pallas_call(
        kernel,
        grid_spec=pltpu.PrefetchScalarGridSpec(
            num_scalar_prefetch=1, grid=(1,),
            in_specs=in_specs or [fixed(x.shape) for x in ins],
            out_specs=[fixed(out.shape) for out in outs]),
        out_shape=outs,
        cost_estimate=pl.CostEstimate(flops=size, transcendentals=0, bytes_accessed=8 * size),
    )(where, *ins)
    return got[:len(shapes)], got[len(shapes):]


def reduce_steps(chunks, group):
    groups = lax.axis_size(DP)
    widths = [grad.shape[1] // part[1] for grad, _, part in chunks]
    if groups != len(RING):
        yield [lax.psum_scatter(grad[:, part[0] * width:part[0] * width + width], DP,
                                scatter_dimension=0, tiled=True).astype(F32)
               for (grad, _, part), width in zip(chunks, widths)]
        return
    rows = chunks[0][0].shape[0] // groups
    bits = (group & 1, (group >> 1) & 1, group >> 2)
    where = jnp.stack(bits)
    axes = [2 - first for _, first, _ in chunks]

    def send(arrays, steps):
        got = []
        for array, step in zip(arrays, steps):
            got.append(flip(array, DP, step))
        return got

    def behind(got, other):
        return got if other is None else list(lax.optimization_barrier((*got, *other))[:len(got)])

    views, aways, gots, specs = [], [], [], []
    for i, (grad, first, part) in enumerate(chunks):
        width = widths[i]
        view = grad.reshape(2, 2, 2, rows, grad.shape[1])
        cut = view[..., part[0] * width:part[0] * width + width]
        aways.append(lax.dynamic_index_in_dim(cut, bits[first] ^ 1, axes[i], keepdims=False))
        views.append(view)
        if first == 0:
            specs.append(pl.BlockSpec((2, 2, 1, rows, width),
                                      lambda i, where, p=part[0]: (0, 0, where[0], 0, p)))
        else:
            specs.append(pl.BlockSpec((2, 1, 2, rows, width),
                                      lambda i, where, p=part[0]: (0, where[1], 0, 0, p)))
    gots = send(aways, [1 << first for _, first, _ in chunks])
    gots = behind(gots, (yield aways))
    specs += [pl.BlockSpec(got.shape, lambda i, where: (0, 0, 0, 0)) for got in gots]
    homes, aways = halve(functools.partial(first_half_kernel, axes), where, [*views, *gots], specs,
                         [(2, rows, width) for width in widths])
    gots = send(aways, [2 >> first for _, first, _ in chunks])
    gots = behind(gots, (yield aways))
    homes, aways = halve(second_half_kernel, where, [*homes, *gots], None,
                         [(rows, width) for width in widths])
    gots = send(aways, [4] * len(chunks))
    gots = behind(gots, (yield aways))
    yield [home + got.astype(F32) for home, got in zip(homes, gots)]


def route_spread(array):
    micro, rows, width = array.shape
    groups = lax.axis_size(DP)
    pieces = array.reshape(micro, groups, rows // groups, width).transpose(1, 0, 2, 3)
    return lax.all_to_all(pieces, DP, split_axis=0, concat_axis=0, tiled=True)


def route_select(held, origin):
    groups, micro, chunk, width = held.shape
    chosen = jnp.take(held.reshape(groups * micro, chunk, width), origin, axis=0, mode=CLIP)
    return chosen.reshape(held.shape)


def route_place(chosen):
    groups, micro, chunk, width = chosen.shape
    home = lax.all_to_all(chosen, DP, split_axis=0, concat_axis=0, tiled=True)
    return home.transpose(1, 0, 2, 3).reshape(micro, groups * chunk, width)


def pad_lanes(array):
    return jnp.pad(array, ((0, 0), (0, LANES - array.shape[1])))


def shards(
    tokens,
    cotangent,
    lengths,
    order,
    proj_gate,
    proj_values,
    proj_delta,
    proj_state,
    proj_out,
    pre_gain,
    gate_gain,
    value_conv,
    value_shift,
    state_conv,
    state_shift,
    delta_bias,
    decay_log,
    skip_gain,
):
    micro, rows, width = tokens.shape
    parts = lax.axis_size(TP)
    part_index = lax.axis_index(TP)
    group = lax.axis_index(DP)
    own_width = proj_gate.shape[1]
    heads = delta_bias.shape[0]
    states = proj_state.shape[1]
    inner_total = own_width * parts
    near_part = part_index ^ jnp.arange(parts, dtype=jnp.int32)
    perm = (near_part >> 1) | ((near_part & 1) << 1)
    slot_ids = jnp.arange(order.shape[0], dtype=jnp.int32)
    inverse = jnp.sum(jnp.where(order[None, :] == slot_ids[:, None], slot_ids[None, :], 0), axis=1)
    local_slots = group * micro + jnp.arange(micro, dtype=jnp.int32)
    lengths_here = jnp.take(lengths, local_slots, mode=CLIP)

    part_of = part_index ^ (jnp.arange(parts, dtype=jnp.int32) >> 1
                            | (jnp.arange(parts, dtype=jnp.int32) & 1) << 1)
    taps = jnp.concatenate([value_conv, state_conv], axis=0).T
    shift = jnp.concatenate([value_shift, state_shift])[None, :]
    bias = pad_lanes(delta_bias[None, :])
    rate = pad_lanes(-jnp.exp(decay_log)[None, :])
    skip = jnp.repeat(skip_gain, own_width // heads)[None, :]
    gain = gate_gain[None, :]
    place = (jnp.arange(own_width)[:, None] // (own_width // heads)
             == jnp.arange(LANES)[None, :]).astype(BF16)
    spread = jnp.concatenate([place.T, place.T], axis=0)

    cot_held = route_spread(cotangent)
    cot_chosen = route_select(cot_held, inverse)
    own = tokens.astype(F32)
    scale = lax.rsqrt(jnp.mean(own * own, axis=-1, keepdims=True) + norm_eps)
    normed = (own * scale * pre_gain).astype(BF16).reshape(micro * rows, width)
    all_rows = gather_rows(normed)

    delta_pad = jnp.pad(proj_delta, ((0, 0), (0, LANES - heads)))
    own_all = jnp.concatenate([proj_values, proj_state, delta_pad, proj_gate, proj_out], axis=1)
    vsd_width = own_width + states + LANES
    ready = (taps, shift, bias, rate, skip, gain, place, spread,
             perm, part_of, lengths_here)
    if lax.axis_size(DP) == len(RING):
        shares, where = ring_pieces(own_all, group, ready, all_rows[1:3])
        chosen = after(cot_chosen, shares[len(RING) - 1], shares[-1])
        own_cot = route_place(chosen)
    else:
        shares = [lax.all_gather(own_all, DP, axis=0, tiled=True)]
        where = jnp.zeros((1,), jnp.int32)
        own_cot = route_place(cot_chosen)
    vsd, gate_in, all_normed, full_in, full_out = project(
        all_rows, shares, where, vsd_width + own_width, vsd_width)
    cot_rows = gather_rows(after(own_cot, vsd).reshape(micro * rows, width))
    mixed, hid, sq, kept = mixer_forward(perm, micro, vsd, gate_in, taps, shift,
                                         bias, rate, skip, gain, spread)
    branch_away, branch_home = branch_rows(hid, full_out)
    branch = scatter_rows(branch_away, branch_home, micro)
    g_hidden, dots, all_cot = hidden_grad(part_of, micro, lengths_here, cot_rows, full_out,
                                          after(hid, branch_home))
    stats = sum_rows(jnp.stack([sq[::8], dots[::8]]))
    g_mixed, low_gate, hidden, gain_sum = gate_backward(
        part_of, micro, inner_total, lengths_here, mixed, gate_in, g_hidden, stats, gain)

    own_chunks = micro * rows // CHUNK
    own_sq = stats[0, :own_chunks].reshape(micro, rows, 1)
    own_r = lax.rsqrt(own_sq / inner_total + norm_eps)
    own_pos = part_index * rows + jnp.arange(rows, dtype=jnp.int32)
    valid = (own_pos[None, :] < lengths_here[:, None]).astype(F32)[:, :, None]
    grad_out = jnp.einsum(ROWS, all_cot, hidden, preferred_element_type=F32).astype(BF16)
    grad_gate = jnp.einsum(ROWS, all_normed, low_gate,
                           preferred_element_type=F32).astype(BF16)
    out_here = jnp.stack([
        (own[slot] + valid[slot] * (add_terms(branch[slot], low_gate) * own_r[slot])).astype(BF16)
        for slot in range(micro)])
    out_held = route_spread(out_here)
    g_mixed = after(g_mixed, out_here, grad_out, grad_gate)
    for early in reduce_steps([(grad_gate, 0, (0, 1)), (grad_out, 1, (0, 1))], group):
        pass
    grad_gate, grad_out = early

    low_vsd, wide, head, pre, g_normed = None, 0.0, 0.0, 0.0, []
    for slot in range(micro):
        low_vsd, wide_part, head_part = mixer_backward(
            perm, micro, slot, vsd, g_mixed, kept, taps, shift, bias, rate, skip, place, spread,
            low_vsd)
        wide, head = wide + wide_part, head + head_part
        if slot == micro - 1:
            grad_state = jnp.einsum(ROWS, all_normed, low_vsd[:, own_width:],
                                    preferred_element_type=F32).astype(BF16)
            grad_values = jnp.einsum(ROWS, after(all_normed, grad_state),
                                     low_vsd[:, :own_width],
                                     preferred_element_type=F32).astype(BF16)
            low_vsd = after(low_vsd, grad_values, grad_state)
        away, home, pre_part = input_grad(micro, slot, low_vsd, low_gate, all_normed, full_in)
        pre = pre + pre_part
        if slot < micro - 1:
            g_normed.append(add_terms(scatter_rows(away, home, 1)[0]))
        if slot == 0:
            out_tokens = route_place(route_select(after(out_held, home), order))
        low_vsd = after(low_vsd, home)

    sums = reduce_steps([(grad_state, 0, (0, 1)), (grad_values, 1, (0, 2)), (grad_values, 0, (1, 2))],
                        group)
    grad_pre = (jnp.sum(pre, axis=0) / pre_gain).reshape(-1, LANES)
    small = jnp.concatenate([wide.reshape(-1, LANES), head[:2], gain_sum[0].reshape(-1, LANES),
                             grad_pre], axis=0)
    late = next(sums)
    if lax.axis_size(DP) == len(RING):
        late = sums.send((home,))
        terms = scatter_rows(away, home, 1, *late)[0]
        small = after(small, terms[3])
        small = small + flip(small, DP, 1)
        late = sums.send((small, out_tokens))
        small = after(small, *late)
        small = small + flip(small, DP, 2)
        small = small + flip(small, DP, 4)
        g_normed.append(add_terms(terms, small))
    else:
        small = sum_over(small, DP)
        g_normed.append(add_terms(scatter_rows(away, home, 1)[0]))
    g_normed = jnp.stack(g_normed)
    gained = g_normed * pre_gain
    grad_own = scale * gained - own * scale**3 * jnp.sum(gained * own, axis=-1,
                                                         keepdims=True) / width
    grad_tokens = (own_cot.astype(F32) + grad_own).astype(BF16)

    small = jnp.concatenate(gather_rows(after(small, grad_tokens), True), axis=0)
    if lax.axis_size(DP) == len(RING):
        late = sums.send((small,))
    grad_vsd = late[0]
    grad_values = jnp.concatenate(late[1:], axis=1)
    own_state, near_state, side_state, far_state = gather_rows(grad_vsd[:, :states], True)
    grad_state = (own_state + near_state) + (side_state + far_state)
    grad_delta = grad_vsd[:, states:states + heads]

    small = jnp.take(small.reshape((parts, -1, LANES)), perm, axis=0, mode=CLIP)
    full = own_width + states
    count = wide.size // LANES
    wides = small[:, :count].reshape(parts, 8, full)
    heads_sum = small[:, count:count + 2]
    gains = small[:, count + 2:count + 2 + own_width // LANES].reshape(parts * own_width)
    state_sum = jnp.sum(wides[:, :5, own_width:], axis=0)
    pre_sum = jnp.sum(small[:, count + 2 + own_width // LANES:], axis=0).reshape(width)
    skip_sum = wides[:, 5, :own_width].reshape(parts * heads, own_width // heads).sum(axis=1)
    return (
        out_tokens,
        grad_tokens,
        grad_gate,
        grad_values,
        grad_delta,
        grad_state,
        grad_out,
        pre_sum,
        gains,
        wides[:, :4, :own_width].transpose(0, 2, 1).reshape(parts * own_width, 4),
        wides[:, 4, :own_width].reshape(parts * own_width),
        state_sum[:4].T,
        state_sum[4],
        heads_sum[:, 0, :heads].reshape(parts * heads),
        heads_sum[:, 1, :heads].reshape(parts * heads),
        skip_sum,
    )


def solution(mesh):
    placed = (
        P(DP, TP, None),
        P(DP, TP, None),
        P(),
        P(),
        P(DP, TP),
        P(DP, TP),
        P(DP, TP),
        P(DP, None),
        P(DP, TP),
        P(),
        P(TP),
        P(TP, None),
        P(TP),
        P(),
        P(),
        P(TP),
        P(TP),
        P(TP),
    )

    return jax.shard_map(
        shards,
        mesh=mesh,
        in_specs=placed,
        out_specs=(
            P(DP, TP, None),
            P(DP, TP, None),
            P(DP, TP),
            P(DP, TP),
            P(DP, TP),
            P(DP, None),
            P(DP, TP),
            P(),
            P(),
            P(),
            P(),
            P(),
            P(),
            P(),
            P(),
            P(),
        ),
        check_vma=False,
    )
```
